512 devices in a mesh: dp: 8 (over z_lo), expert: 64 (over z_hi, y, x, core).
Axes of the slice: x: 4, y: 4, z: 16 (z_hi: 2, z_lo: 8; z = z_hi * 8 + z_lo), core: 2. Of those that a mesh axis runs over, the one named last changes fastest.
Arguments:
- route_ids: int32 [8192, 8], P(('dp', 'expert')), may hold values from 0 to 63, all different within a row; in each aligned block of 16 rows (0 to 15, 16 to 31, ...) at most 4 rows name the same one
- route_probs: float32 [8192, 8], P(('dp', 'expert')), may hold values from 0.02 to 0.25
- hidden: bfloat16 [8192, 8, 768], P(('dp', 'expert')), may hold values from -6 to 6
- upstream: bfloat16 [8192, 2048], P(('dp', 'expert')), may hold values from -6 to 6
- placement: int32 [64], replicated, may hold values from 0 to 63, each once
- swap_flags: int32 [64], replicated, may hold values from 0 to 1, as said below
- weights: bfloat16 [64, 768, 2048], P('expert', 'dp'), may hold values from -0.21875 to 0.21875
- moment1: float32 [64, 768, 2048], P('expert', 'dp'), may hold values from -24 to 24
- moment2: float32 [64, 768, 2048], P('expert', 'dp'), may hold values from 4 to 100
Outputs:
- layer_out: bfloat16 [8192, 2048], P(('dp', 'expert'))
- hidden_grads: bfloat16 [8192, 8, 768], P(('dp', 'expert'))
- new_weights: bfloat16 [64, 768, 2048], P('expert', 'dp')
- new_moment1: float32 [64, 768, 2048], P('expert', 'dp')
- new_moment2: float32 [64, 768, 2048], P('expert', 'dp')
The draws below stay inside these ranges and needn't reach their ends.
Inputs may be any that keep to these rules, and one draw needn't show every extreme that they name: `route_ids`: within the rows of one device no expert is named more than 4 times, a bound that some block reaches. `placement`: A permutation of the expert-axis indices. swap_flags[i] equals swap_flags[(i + 32) mod 64], so trades are mutual between indices half the axis apart; swap_flags[0] and swap_flags[31] are 1.
All inputs are finite; a program needn't handle non-finite values.
Results may differ from the reference program's by a relative error of at most 0.006.
Values may be sent and summed in bfloat16 or wider, within the bound.
No kernel may reach another device: no remote copies, remote signals or barrier semaphores. Data moves between devices by JAX's collectives and lax.ppermute only.
A program may use at most 64 MiB of HBM per device.

```python
import math
import jax
import jax.numpy as jnp
import numpy as np
from jax import lax

D = 2048
H = 768
TOP = 8
TOK_DEV = 16
EXPERTS = 64
CAP = 4
TOKENS = 8192
N_DP = 8


def draw_swap_flags(key, part):
    lower_half = jax.random.randint(key, (EXPERTS // 2,), 0, 2, dtype=jnp.int32)
    lower_half = lower_half.at[0].set(1)
    lower_half = lower_half.at[EXPERTS // 2 - 1].set(1)
    return jnp.concatenate([lower_half, lower_half])


def steps_of(stream_key, dims, pieces, smallest, largest):
    gain = 1.0
    for axis_at, parts in pieces:
        heights = jax.random.uniform(jax.random.fold_in(jax.random.fold_in(stream_key, 6), axis_at), (parts,), jnp.float32, smallest / len(pieces), largest / len(pieces))
        gain = gain * jnp.repeat(jnp.exp(heights), dims[axis_at] // parts).reshape((-1,) + (1,) * (len(dims) - 1 - axis_at))
    return gain


def routed_block(rng, own, number, rows, number_of, top, most, skew):
    order = jax.random.permutation(rng, number_of)
    crowded, usual = portions_of(number_of, rows * top, most, skew, True), portions_of(number_of, rows * top, most, skew, False)
    places = jnp.arange(number_of)

    def named(sizes, turn):
        used = int((sizes > 0).sum())
        fixed = max(1, used // 4)
        shifted = fixed + (places - fixed + turn * (used - fixed)) % max(1, number_of - fixed)
        return jnp.zeros((number_of,), jnp.int32).at[order[jnp.where(places < fixed, places, shifted)]].set(jnp.asarray(sizes, jnp.int32))

    sizes = jnp.where(number % 4 == 0, named(crowded, number // 4), named(usual, number - number // 4 - 1))
    mixed = jax.random.permutation(jax.random.fold_in(own, 3), number_of)
    giver, sink = mixed[0:number_of // 2 * 2:2], mixed[1:number_of // 2 * 2:2]
    margin = jnp.minimum(sizes[giver] - 1, most - sizes[sink]) // 2
    margin = jnp.where((giver == order[0]) | (sink == order[0]) | (sizes[sink] == 0), 0, jnp.maximum(margin, 0))
    shifted = jax.random.randint(jax.random.fold_in(own, 4), (number_of // 2,), 0, 1 << 20) % (margin + 1)
    sizes = sizes.at[giver].add(-shifted).at[sink].add(shifted)
    members = jnp.searchsorted(jnp.cumsum(sizes), jnp.arange(rows * top), side="right").astype(jnp.int32)
    grid = members.reshape(top, rows).T
    grid = grid[jax.random.permutation(jax.random.fold_in(own, 1), rows)]
    turn = jax.random.randint(jax.random.fold_in(own, 2), (rows, 1), 0, top)
    return jnp.take_along_axis(grid, (jnp.arange(top)[None, :] + turn) % top, axis=1)


def portions_of(amount, total, reach, slope, full):
    portions = [(1 << 20) // math.isqrt(standing ** slope) + 1 for standing in range(1, amount + 1)]
    largest = reach if full else min(reach, max(-(-total // amount), total * portions[0] // sum(portions)))
    least = 1 if total - largest >= amount - 1 else 0
    given, surplus = [largest] + [least] * (amount - 1), total - largest - least * (amount - 1)
    while surplus > 0:
        free = [i for i in range(1, amount) if given[i] < largest] or [i for i in range(1, amount) if given[i] < reach]
        mass, budget = sum([portions[i] for i in free]), surplus
        for i in free:
            extra = min(reach - given[i], max(1, budget * portions[i] // mass), surplus)
            given[i] = given[i] + extra
            surplus = surplus - extra
    return np.array(given)


def normal_values(stream_key, dims, spread, bound, pieces=(), kind=jnp.bfloat16):
    loudness = steps_of(stream_key, dims, pieces, -0.22, 0.18) if pieces else 1.0
    drawn = jax.random.normal(stream_key, dims, jnp.float32) * spread * loudness
    return jnp.minimum(jnp.maximum(drawn, -bound), bound).astype(kind)


def setup_inputs(seed: int = 0) -> dict:
    key_of = jax.random.split(jax.random.key(seed), 10)
    route_ids_keys = jax.random.split(jax.random.fold_in(key_of[0], 1), TOKENS // TOK_DEV)
    route_ids_turns = jax.random.permutation(jax.random.fold_in(key_of[0], 3), TOKENS // TOK_DEV)
    route_ids = jax.vmap(lambda own, number: routed_block(jax.random.fold_in(key_of[0], 2), own, number, TOK_DEV, EXPERTS, TOP, CAP, 2))(route_ids_keys, route_ids_turns).reshape((TOKENS, TOP))
    route_probs = jnp.clip(0.02 + 0.23 * jax.random.uniform(key_of[1], (TOKENS, TOP), jnp.float32) ** steps_of(key_of[1], (TOKENS, TOP), ((0, 512),), -0.2, 0.2), 0.02, 0.25)
    hidden = normal_values(key_of[2], (TOKENS, TOP, H), 1.0, 6.0, ((0, 512),))
    upstream = normal_values(key_of[3], (TOKENS, D), 1.0, 6.0, ((0, 512),))
    placement = jax.random.permutation(key_of[4], EXPERTS).astype(jnp.int32)
    swap_flags = draw_swap_flags(jax.random.fold_in(key_of[9], 71), 0)
    weights = normal_values(key_of[6], (EXPERTS, H, D), H ** -0.5, 0.21875, ((0, 64), (1, 8)))
    moment1 = normal_values(key_of[7], (EXPERTS, H, D), 4.0, 24.0, ((0, 64), (1, 8)), jnp.float32)
    moment2 = jnp.clip(jnp.exp(math.log(100.0) - 3.218876 * jax.random.uniform(key_of[8], (EXPERTS, H, D), jnp.float32) ** steps_of(key_of[8], (EXPERTS, H, D), ((0, 64), (1, 8)), -0.2, 0.2)), 4.0, 100.0)
    return {"route_ids": route_ids, "route_probs": route_probs, "hidden": hidden, "upstream": upstream, "placement": placement, "swap_flags": swap_flags, "weights": weights, "moment1": moment1, "moment2": moment2}


decay_one = 0.9
decay_two = 0.95
learn_rate = 0.01
bias_one = 1.0 - 0.9 ** 10
bias_two = 1.0 - 0.95 ** 10
epsilon = 1e-08

def adam_update(weight, first, second, gradient):
    new_first = decay_one * first + (1.0 - decay_one) * gradient
    new_second = decay_two * second + (1.0 - decay_two) * gradient * gradient
    step_size = learn_rate * (new_first / bias_one) / (jnp.sqrt(new_second / bias_two) + epsilon)
    return ((weight.astype(jnp.float32) - step_size).astype(jnp.bfloat16), new_first, new_second)

def reference(route_ids, route_probs, hidden, upstream, placement, swap_flags, weights, moment1, moment2):
    half_way = EXPERTS // 2
    total_rows = TOKENS * TOP
    group_rows = CAP * EXPERTS
    flat_ids = route_ids.reshape(-1).astype(jnp.int32)
    row_token = (jnp.arange(total_rows, dtype=jnp.int32) // TOP).astype(jnp.int32)
    row_replica = (row_token // (TOK_DEV * EXPERTS)).astype(jnp.int32)
    group_key = (flat_ids * N_DP + row_replica).astype(jnp.int32)
    sort_order = jnp.argsort(group_key, stable=True).astype(jnp.int32)
    counts = jnp.zeros((EXPERTS * N_DP,), jnp.int32).at[group_key].add(1)
    starts = (jnp.cumsum(counts) - counts).astype(jnp.int32)
    sorted_hidden = jnp.concatenate([hidden.reshape(total_rows, H)[sort_order], jnp.zeros((group_rows, H), hidden.dtype)])
    sorted_token = jnp.concatenate([row_token[sort_order], jnp.zeros((group_rows,), jnp.int32)])
    sorted_prob = jnp.concatenate([route_probs.reshape(-1)[sort_order], jnp.zeros((group_rows,), route_probs.dtype)])
    expert_weights = weights[placement]
    row_iota = jnp.arange(group_rows, dtype=jnp.int32)

    def expert_step(carry, inputs):
        mixed_acc, grad_store = carry
        expert_id, weight_e = inputs

        def group_step(inner, replica):
            mixed_inner, grad_inner, gradient = inner
            slot = expert_id * N_DP + replica
            first_row = starts[slot]
            live_count = counts[slot]
            block_h = lax.dynamic_slice_in_dim(sorted_hidden, first_row, group_rows, 0)
            block_tok = lax.dynamic_slice_in_dim(sorted_token, first_row, group_rows, 0)
            block_prob = lax.dynamic_slice_in_dim(sorted_prob, first_row, group_rows, 0)
            live_rows = row_iota < live_count
            product = jnp.dot(block_h, weight_e, preferred_element_type=jnp.float32).astype(jnp.bfloat16)
            contribution = jnp.where(live_rows[:, None], block_prob[:, None] * product.astype(jnp.float32), 0.0)
            mixed_inner = mixed_inner.at[block_tok].add(contribution)
            scaled = (block_prob[:, None] * upstream[block_tok].astype(jnp.float32)).astype(jnp.bfloat16)
            scaled = jnp.where(live_rows[:, None], scaled, jnp.zeros_like(scaled))
            back_rows = jnp.dot(scaled, weight_e.T, preferred_element_type=jnp.float32).astype(jnp.bfloat16)
            current = lax.dynamic_slice_in_dim(grad_inner, first_row, group_rows, 0)
            grad_inner = lax.dynamic_update_slice_in_dim(grad_inner, jnp.where(live_rows[:, None], back_rows, current), first_row, 0)
            partial_sum = lax.dot_general(block_h, scaled, (((0,), (0,)), ((), ())), preferred_element_type=jnp.float32)
            rounded = lax.optimization_barrier(partial_sum.astype(jnp.bfloat16))
            gradient = gradient + rounded.astype(jnp.float32)
            return ((mixed_inner, grad_inner, gradient), None)
        start_state = (mixed_acc, grad_store, jnp.zeros((H, D), jnp.float32))
        (mixed_acc, grad_store, gradient), _ = lax.scan(group_step, start_state, jnp.arange(N_DP, dtype=jnp.int32))
        return ((mixed_acc, grad_store), gradient)
    start_carry = (jnp.zeros((TOKENS, D), jnp.float32), jnp.zeros((total_rows + group_rows, H), jnp.bfloat16))
    (mixed_acc, grad_store), gradients = lax.scan(expert_step, start_carry, (jnp.arange(EXPERTS, dtype=jnp.int32), expert_weights))
    layer_out = mixed_acc.astype(jnp.bfloat16)
    hidden_grads = jnp.zeros((total_rows, H), jnp.bfloat16).at[sort_order].set(grad_store[:total_rows]).reshape(TOKENS, TOP, H)
    new_w, new_first, new_second = adam_update(expert_weights, moment1[placement], moment2[placement], gradients)
    new_home = ((placement + swap_flags[placement] * half_way) % EXPERTS).astype(jnp.int32)
    new_weights = jnp.zeros_like(weights).at[new_home].set(new_w)
    new_moment1 = jnp.zeros_like(moment1).at[new_home].set(new_first)
    new_moment2 = jnp.zeros_like(moment2).at[new_home].set(new_second)
    return (layer_out, hidden_grads, new_weights, new_moment1, new_moment2)
```

```python
import jax
import jax.numpy as jnp
from jax import lax
from jax.sharding import Mesh, PartitionSpec as P

decay_one = 0.9
decay_two = 0.95
learn_rate = 0.01
bias_one = 1.0 - 0.9**10
bias_two = 1.0 - 0.95**10
epsilon = 1e-08


def adam_update(weight, first, second, gradient):
    new_first = decay_one * first + (1.0 - decay_one) * gradient
    new_second = decay_two * second + (1.0 - decay_two) * gradient * gradient
    step_size = learn_rate * (new_first / bias_one) / (jnp.sqrt(new_second / bias_two) + epsilon)
    return ((weight.astype(jnp.float32) - step_size).astype(jnp.bfloat16), new_first, new_second)


def table_lookup(lookup_table, positions):
    iota_slots = jnp.arange(lookup_table.shape[0], dtype=jnp.int32)
    matches = positions[..., None] == iota_slots
    return jnp.sum(jnp.where(matches, lookup_table, 0), axis=-1)


def shards(
    route_ids, route_probs, hidden, upstream, placement, swap_flags, weights, moment1, moment2
):
    plane = lax.axis_size("p")
    my_half, my_place, my_dp = lax.axis_index("zh"), lax.axis_index("p"), lax.axis_index("dp")
    tokens_here, chosen = route_ids.shape
    width = upstream.shape[1]
    hidden_width = hidden.shape[2]
    rows_dp = weights.shape[1]
    total_rows = tokens_here * chosen
    capacity = total_rows // plane
    slots = 2 * capacity
    flip_mine = table_lookup(swap_flags, my_place)

    across = [(0, 1), (1, 0)]
    first_far = lax.ppermute(moment1.astype(jnp.bfloat16), "zh", across)
    second_far = lax.ppermute(moment2.astype(jnp.bfloat16), "zh", across)
    full_weights = lax.all_gather(weights[0], ("zh", "dp"), axis=0, tiled=True)

    target = table_lookup(placement, route_ids.reshape(-1))
    slot_iota = jnp.arange(2 * plane, dtype=jnp.int32)
    onehot = (target[:, None] == slot_iota[None, :]).astype(jnp.int32)
    rank = jnp.sum((jnp.cumsum(onehot, axis=0) - onehot) * onehot, axis=1)
    position = (target % plane) * slots + (target // plane) * capacity + rank

    send_hidden = jnp.zeros((plane * slots, hidden_width), jnp.bfloat16)
    send_hidden = send_hidden.at[position].set(hidden.reshape(total_rows, hidden_width))
    send_hidden = send_hidden.reshape(plane, slots, hidden_width)
    got_hidden = lax.all_to_all(send_hidden, "p", split_axis=0, concat_axis=0, tiled=True)
    scaled = (route_probs[..., None] * upstream[:, None, :].astype(jnp.float32)).astype(
        jnp.bfloat16
    )
    send_grads = jnp.zeros((plane * slots, width), jnp.bfloat16)
    send_grads = send_grads.at[position].set(scaled.reshape(total_rows, width))
    send_grads = send_grads.reshape(plane, slots, width)
    got_grads = lax.all_to_all(send_grads, "p", split_axis=0, concat_axis=0, tiled=True)

    flat_hidden = got_hidden.reshape(plane * slots, hidden_width)
    flat_grads = got_grads.reshape(plane * slots, width)
    half = (jnp.arange(plane * slots, dtype=jnp.int32) // capacity % 2)[:, None]
    zero = jnp.zeros_like(flat_hidden)
    spread = jnp.concatenate(
        [jnp.where(half == 0, flat_hidden, zero), jnp.where(half == 1, flat_hidden, zero)], axis=1
    )
    new_half = half ^ flip_mine
    spread_new = jnp.concatenate(
        [jnp.where(new_half == 0, flat_hidden, zero), jnp.where(new_half == 1, flat_hidden, zero)],
        axis=1,
    )
    partial = lax.dot_general(
        spread_new, flat_grads, (((0,), (0,)), ((), ())), preferred_element_type=jnp.float32
    ).astype(jnp.bfloat16)
    gradient = lax.psum_scatter(
        partial, ("zh", "dp"), scatter_dimension=0, tiled=True
    ).astype(jnp.float32)

    terms = jnp.dot(spread, full_weights, preferred_element_type=jnp.float32).astype(jnp.bfloat16)
    back_terms = lax.all_to_all(
        terms.reshape(plane, slots, width), "p", split_axis=0, concat_axis=0, tiled=True
    )
    both = lax.dot_general(
        flat_grads, full_weights, (((1,), (1,)), ((), ())), preferred_element_type=jnp.float32
    ).astype(jnp.bfloat16)
    row_grads = jnp.where(half == 0, both[:, :hidden_width], both[:, hidden_width:])
    back_grads = lax.all_to_all(
        row_grads.reshape(plane, slots, hidden_width), "p", split_axis=0, concat_axis=0, tiled=True
    )
    expert_terms = back_terms.reshape(plane * slots, width)[position].reshape(
        tokens_here, chosen, width
    )
    layer_out = jnp.sum(route_probs[..., None] * expert_terms.astype(jnp.float32), axis=1).astype(
        jnp.bfloat16
    )
    hidden_grads = back_grads.reshape(plane * slots, hidden_width)[position].reshape(
        tokens_here, chosen, hidden_width
    )

    old_half = my_half ^ flip_mine
    weight_here = lax.dynamic_slice_in_dim(
        full_weights, old_half * hidden_width + my_dp * rows_dp, rows_dp, 0
    )
    first_here = jnp.where(flip_mine == 1, first_far[0].astype(jnp.float32), moment1[0])
    second_here = jnp.where(flip_mine == 1, second_far[0].astype(jnp.float32), moment2[0])
    new_w, new_first, new_second = adam_update(weight_here, first_here, second_here, gradient)
    return (layer_out, hidden_grads, new_w[None], new_first[None], new_second[None])


def solution(mesh):
    n_dp, n_expert = mesh.shape["dp"], mesh.shape["expert"]
    mesh = Mesh(mesh.devices.reshape(n_dp, 2, n_expert // 2), ("dp", "zh", "p"))
    tokens, experts = ("dp", "zh", "p"), ("zh", "p")
    in_specs = (
        P(tokens, None),
        P(tokens, None),
        P(tokens, None, None),
        P(tokens, None),
        P(),
        P(),
        P(experts, "dp", None),
        P(experts, "dp", None),
        P(experts, "dp", None),
    )
    out_specs = (
        P(tokens, None),
        P(tokens, None, None),
        P(experts, "dp", None),
        P(experts, "dp", None),
        P(experts, "dp", None),
    )
    return jax.shard_map(shards, mesh=mesh, in_specs=in_specs, out_specs=out_specs, check_vma=False)
```

```python
import jax
import jax.numpy as jnp
from jax import lax
from jax.experimental import pallas as pl
from jax.experimental.pallas import tpu as pltpu
from jax.sharding import Mesh, PartitionSpec as P

decay_one = 0.9
decay_two = 0.95
learn_rate = 0.01
bias_one = 1.0 - 0.9**10
bias_two = 1.0 - 0.95**10
epsilon = 1e-08


LANES, STEP = 128, 4


def adam_update(weight, first, second, gradient):
    new_first = decay_one * first + (1.0 - decay_one) * gradient
    new_second = decay_two * second + (1.0 - decay_two) * gradient * gradient
    step_size = learn_rate * (new_first / bias_one) / (jnp.sqrt(new_second / bias_two) + epsilon)
    return ((weight.astype(jnp.float32) - step_size).astype(jnp.bfloat16), new_first, new_second)


def pack_kernel(first_ref, second_ref, out_ref):
    for block in range(out_ref.shape[1]):
        columns = pl.ds(block * LANES, LANES)
        out_ref[0, block] = first_ref[0, :, columns].astype(jnp.bfloat16)
        out_ref[1, block] = second_ref[0, :, columns].astype(jnp.bfloat16)


def pack_moments(first, second):
    _, rows, width = first.shape
    blocks = width // LANES
    step = STEP if blocks % STEP == 0 else 1
    moment = pl.BlockSpec((1, rows, step * LANES), lambda i: (0, 0, i))
    return pl.pallas_call(
        pack_kernel,
        grid=(blocks // step,),
        in_specs=[moment, moment],
        out_specs=pl.BlockSpec((2, step, rows, LANES), lambda i: (0, i, 0, 0)),
        out_shape=jax.ShapeDtypeStruct((2, blocks, rows, LANES), jnp.bfloat16),
    )(first, second)


def adam_kernel(
    where_ref, weight_ref, gradient_ref, first_ref, second_ref, far_ref, w_ref, m_ref, v_ref
):
    moved = where_ref[1] == 1
    for block in range(far_ref.shape[1]):
        columns = pl.ds(block * LANES, LANES)
        first = jnp.where(moved, far_ref[0, block].astype(jnp.float32), first_ref[0, :, columns])
        second = jnp.where(moved, far_ref[1, block].astype(jnp.float32), second_ref[0, :, columns])
        w_ref[0, :, columns], m_ref[0, :, columns], v_ref[0, :, columns] = adam_update(
            weight_ref[:, columns], first, second, gradient_ref[:, columns].astype(jnp.float32)
        )


def adam_step(row_block, moved, full_weights, gradient, first, second, far):
    _, rows, width = first.shape
    blocks = width // LANES
    step = STEP if blocks % STEP == 0 else 1
    state = pl.BlockSpec((1, rows, step * LANES), lambda i, where: (0, 0, i))
    grid_spec = pltpu.PrefetchScalarGridSpec(
        num_scalar_prefetch=1,
        grid=(blocks // step,),
        in_specs=[
            pl.BlockSpec((rows, step * LANES), lambda i, where: (where[0], i)),
            pl.BlockSpec((rows, step * LANES), lambda i, where: (0, i)),
            state,
            state,
            pl.BlockSpec((2, step, rows, LANES), lambda i, where: (0, i, 0, 0)),
        ],
        out_specs=[state, state, state],
    )
    return pl.pallas_call(
        adam_kernel,
        grid_spec=grid_spec,
        out_shape=[
            jax.ShapeDtypeStruct(first.shape, jnp.bfloat16),
            jax.ShapeDtypeStruct(first.shape, jnp.float32),
            jax.ShapeDtypeStruct(first.shape, jnp.float32),
        ],
    )(jnp.stack([row_block, moved]), full_weights, gradient, first, second, far)


def table_lookup(lookup_table, positions):
    iota_slots = jnp.arange(lookup_table.shape[0], dtype=jnp.int32)
    matches = positions[..., None] == iota_slots
    return jnp.sum(jnp.where(matches, lookup_table, 0), axis=-1)


def shards(
    route_ids, route_probs, hidden, upstream, placement, swap_flags, weights, moment1, moment2
):
    plane = lax.axis_size("p")
    my_half, my_place, my_dp = lax.axis_index("zh"), lax.axis_index("p"), lax.axis_index("dp")
    tokens_here, chosen = route_ids.shape
    width = upstream.shape[1]
    hidden_width = hidden.shape[2]
    rows_dp = weights.shape[1]
    total_rows = tokens_here * chosen
    capacity = total_rows // plane
    slots = 2 * capacity
    flip_mine = table_lookup(swap_flags, my_place)

    plane_flags = swap_flags[:plane]
    order = jnp.cumsum(plane_flags) - 1
    trading = order[-1] + 1
    lines = jnp.arange(plane, dtype=jnp.int32)
    taken = (order[None, :] == lines[:, None]) & (plane_flags[None, :] == 1)
    nth = jnp.sum(jnp.where(taken, lines[None, :], 0), axis=1)
    order = jnp.maximum(order, 0)
    sizes = sorted({max(1, plane * part // 32) for part in (8, 12, 14, 16, 18, 20, 22, 24, 28, 32)})
    chosen_size = sum((trading > size).astype(jnp.int32) for size in sizes[:-1])

    def crossing(size):
        def branch(blocks):
            packed = jnp.take(blocks, nth[:size], axis=0, mode="clip")
            packed = lax.ppermute(packed, "zh", [(0, 1), (1, 0)])
            return jnp.take(packed, order, axis=0, mode="clip")

        return branch

    def cross(blocks):
        return lax.switch(chosen_size, [crossing(size) for size in sizes], blocks)

    moment_blocks = pack_moments(moment1, moment2)
    spread_blocks = lax.all_to_all(
        moment_blocks.reshape(plane, -1, rows_dp, LANES), "p", split_axis=0, concat_axis=0, tiled=True
    )
    mine = spread_blocks.shape[1]
    spread_blocks = spread_blocks.reshape(plane, mine * rows_dp, LANES)
    cut = mine * rows_dp // 2
    early_far = cross(spread_blocks[:, :cut])
    hidden, upstream, _ = lax.optimization_barrier((hidden, upstream, early_far))
    full_weights = lax.all_gather(weights[0], ("zh", "dp"), axis=0, tiled=True)

    target = table_lookup(placement, route_ids.reshape(-1))
    slot_iota = jnp.arange(2 * plane, dtype=jnp.int32)
    onehot = (target[:, None] == slot_iota[None, :]).astype(jnp.int32)
    rank = jnp.sum((jnp.cumsum(onehot, axis=0) - onehot) * onehot, axis=1)
    position = (target % plane) * slots + (target // plane) * capacity + rank

    send_hidden = jnp.zeros((plane * slots, hidden_width), jnp.bfloat16)
    send_hidden = send_hidden.at[position].set(hidden.reshape(total_rows, hidden_width))
    send_hidden = send_hidden.reshape(plane, slots, hidden_width)
    got_hidden = lax.all_to_all(send_hidden, "p", split_axis=0, concat_axis=0, tiled=True)
    scaled = (route_probs[..., None] * upstream[:, None, :].astype(jnp.float32)).astype(
        jnp.bfloat16
    )
    send_grads = jnp.zeros((plane * slots, width), jnp.bfloat16)
    send_grads = send_grads.at[position].set(scaled.reshape(total_rows, width))
    send_grads = send_grads.reshape(plane, slots, width)
    got_grads = lax.all_to_all(send_grads, "p", split_axis=0, concat_axis=0, tiled=True)

    flat_hidden = got_hidden.reshape(plane * slots, hidden_width)
    flat_grads = got_grads.reshape(plane * slots, width)
    half = (jnp.arange(plane * slots, dtype=jnp.int32) // capacity % 2)[:, None]
    zero = jnp.zeros_like(flat_hidden)
    spread = jnp.concatenate(
        [jnp.where(half == 0, flat_hidden, zero), jnp.where(half == 1, flat_hidden, zero)], axis=1
    )
    new_half = half ^ flip_mine
    spread_new = jnp.concatenate(
        [jnp.where(new_half == 0, flat_hidden, zero), jnp.where(new_half == 1, flat_hidden, zero)],
        axis=1,
    )
    partial = lax.dot_general(
        spread_new, flat_grads, (((0,), (0,)), ((), ())), preferred_element_type=jnp.float32
    ).astype(jnp.bfloat16)
    gradient = lax.psum_scatter(
        partial, ("zh", "dp"), scatter_dimension=0, tiled=True
    )
    full_weights, _ = lax.optimization_barrier((full_weights, partial))

    terms = jnp.dot(spread, full_weights, preferred_element_type=jnp.float32).astype(jnp.bfloat16)
    back_terms = lax.all_to_all(
        terms.reshape(plane, slots, width), "p", split_axis=0, concat_axis=0, tiled=True
    )
    both = lax.dot_general(
        flat_grads, full_weights, (((1,), (1,)), ((), ())), preferred_element_type=jnp.float32
    ).astype(jnp.bfloat16)
    row_grads = jnp.where(half == 0, both[:, :hidden_width], both[:, hidden_width:])
    back_grads = lax.all_to_all(
        row_grads.reshape(plane, slots, hidden_width), "p", split_axis=0, concat_axis=0, tiled=True
    )
    expert_terms = back_terms.reshape(plane * slots, width)[position].reshape(
        tokens_here, chosen, width
    )
    layer_out = jnp.sum(route_probs[..., None] * expert_terms.astype(jnp.float32), axis=1).astype(
        jnp.bfloat16
    )
    hidden_grads = back_grads.reshape(plane * slots, hidden_width)[position].reshape(
        tokens_here, chosen, hidden_width
    )

    late_blocks, _, _ = lax.optimization_barrier((spread_blocks[:, cut:], terms, row_grads))
    late_far = cross(late_blocks)
    far = jnp.concatenate([early_far, late_far], axis=1).reshape(plane, mine, rows_dp, LANES)
    far = lax.all_to_all(far, "p", split_axis=0, concat_axis=0, tiled=True)
    old_half = my_half ^ flip_mine
    row_block = old_half * (hidden_width // rows_dp) + my_dp
    new_w, new_first, new_second = adam_step(
        row_block, flip_mine, full_weights, gradient, moment1, moment2, far.reshape(moment_blocks.shape)
    )
    return (layer_out, hidden_grads, new_w, new_first, new_second)


def solution(mesh):
    n_dp, n_expert = mesh.shape["dp"], mesh.shape["expert"]
    mesh = Mesh(mesh.devices.reshape(n_dp, 2, n_expert // 2), ("dp", "zh", "p"))
    tokens, experts = ("dp", "zh", "p"), ("zh", "p")
    in_specs = (
        P(tokens, None),
        P(tokens, None),
        P(tokens, None, None),
        P(tokens, None),
        P(),
        P(),
        P(experts, "dp", None),
        P(experts, "dp", None),
        P(experts, "dp", None),
    )
    out_specs = (
        P(tokens, None),
        P(tokens, None, None),
        P(experts, "dp", None),
        P(experts, "dp", None),
        P(experts, "dp", None),
    )
    return jax.shard_map(shards, mesh=mesh, in_specs=in_specs, out_specs=out_specs, check_vma=False)
```

```python
import jax
import jax.numpy as jnp
from jax import lax
from jax.experimental import pallas as pl
from jax.experimental.pallas import tpu as pltpu
from jax.sharding import Mesh, PartitionSpec as P

decay_one = 0.9
decay_two = 0.95
learn_rate = 0.01
bias_one = 1.0 - 0.9**10
bias_two = 1.0 - 0.95**10
epsilon = 1e-08


LANES, STEP = 128, 4
PARTS = (4, 8, 10, 12, 13, 14, 15, 16, 17, 18, 19, 20, 21, 22, 24, 26, 28, 32)


def adam_update(weight, decayed_first, decayed_second, gradient):
    new_first = decayed_first + (1.0 - decay_one) * gradient
    new_second = decayed_second + (1.0 - decay_two) * gradient * gradient
    spread = jnp.sqrt(new_second * (1.0 / bias_two)) + epsilon
    step_size = new_first * (learn_rate / bias_one) / spread
    return ((weight.astype(jnp.float32) - step_size).astype(jnp.bfloat16), new_first, new_second)


def pack_kernel(first_ref, second_ref, out_ref):
    for block in range(out_ref.shape[1]):
        columns = pl.ds(block * LANES, LANES)
        out_ref[0, block] = first_ref[0, :, columns].astype(jnp.bfloat16)
        out_ref[1, block] = second_ref[0, :, columns].astype(jnp.bfloat16)


def pack_moments(first, second):
    _, rows, width = first.shape
    blocks = width // LANES
    step = STEP if blocks % STEP == 0 else 1
    moment = pl.BlockSpec((1, rows, step * LANES), lambda i: (0, 0, i))
    return pl.pallas_call(
        pack_kernel,
        grid=(blocks // step,),
        in_specs=[moment, moment],
        out_specs=pl.BlockSpec((2, step, rows, LANES), lambda i: (0, i, 0, 0)),
        out_shape=jax.ShapeDtypeStruct((2, blocks, rows, LANES), jnp.bfloat16),
    )(first, second)


def home_kernel(where_ref, weight_ref, first_ref, second_ref, far_ref, w_ref, m_ref, v_ref):
    moved = where_ref[1] == 1
    w_ref[0] = weight_ref[...]
    for block in range(far_ref.shape[1]):
        columns = pl.ds(block * LANES, LANES)
        first = jnp.where(moved, far_ref[0, block].astype(jnp.float32), first_ref[0, :, columns])
        second = jnp.where(moved, far_ref[1, block].astype(jnp.float32), second_ref[0, :, columns])
        m_ref[0, :, columns] = decay_one * first
        v_ref[0, :, columns] = decay_two * second


def state_at_home(row_block, moved, full_weights, first, second, far):
    _, rows, width = first.shape
    blocks = width // LANES
    step = STEP if blocks % STEP == 0 else 1
    state = pl.BlockSpec((1, rows, step * LANES), lambda i, where: (0, 0, i))
    grid_spec = pltpu.PrefetchScalarGridSpec(
        num_scalar_prefetch=1,
        grid=(blocks // step,),
        in_specs=[
            pl.BlockSpec((rows, step * LANES), lambda i, where: (where[0], i)),
            state,
            state,
            pl.BlockSpec((2, step, rows, LANES), lambda i, where: (0, i, 0, 0)),
        ],
        out_specs=[state, state, state],
    )
    return pl.pallas_call(
        home_kernel,
        grid_spec=grid_spec,
        out_shape=[
            jax.ShapeDtypeStruct(first.shape, jnp.bfloat16),
            jax.ShapeDtypeStruct(first.shape, jnp.float32),
            jax.ShapeDtypeStruct(first.shape, jnp.float32),
        ],
    )(jnp.stack([row_block, moved]), full_weights, first, second, far)


def table_lookup(lookup_table, positions):
    iota_slots = jnp.arange(lookup_table.shape[0], dtype=jnp.int32)
    matches = positions[..., None] == iota_slots
    return jnp.sum(jnp.where(matches, lookup_table, 0), axis=-1)


def shards(
    route_ids, route_probs, hidden, upstream, placement, swap_flags, weights, moment1, moment2
):
    plane = lax.axis_size("p")
    my_half, my_place, my_dp = lax.axis_index("zh"), lax.axis_index("p"), lax.axis_index("dp")
    tokens_here, chosen = route_ids.shape
    width = upstream.shape[1]
    hidden_width = hidden.shape[2]
    rows_dp = weights.shape[1]
    total_rows = tokens_here * chosen
    capacity = total_rows // plane
    slots = 2 * capacity
    flip_mine = table_lookup(swap_flags, my_place)

    plane_flags = swap_flags[:plane]
    order = jnp.cumsum(plane_flags) - 1
    trading = order[-1] + 1
    lines = jnp.arange(plane, dtype=jnp.int32)
    taken = (order[None, :] == lines[:, None]) & (plane_flags[None, :] == 1)
    nth = jnp.sum(jnp.where(taken, lines[None, :], 0), axis=1)
    order = jnp.maximum(order, 0)
    sizes = sorted({max(1, plane * part // 32) for part in PARTS})
    chosen_size = sum((trading > size).astype(jnp.int32) for size in sizes[:-1])

    def crossing(size):
        def branch(blocks):
            packed = jnp.take(blocks, nth[:size], axis=0, mode="clip")
            packed = lax.ppermute(packed, "zh", [(0, 1), (1, 0)])
            return jnp.take(packed, order, axis=0, mode="clip")

        return branch

    def cross(blocks):
        return lax.switch(chosen_size, [crossing(size) for size in sizes], blocks)

    moment_blocks = pack_moments(moment1, moment2)
    spread_blocks = lax.all_to_all(
        moment_blocks.reshape(plane, -1, rows_dp, LANES), "p", split_axis=0, concat_axis=0, tiled=True
    )
    mine = spread_blocks.shape[1]
    spread_blocks = spread_blocks.reshape(plane, mine * rows_dp, LANES)
    cut = mine * rows_dp // 2
    early_far = cross(spread_blocks[:, :cut])
    hidden, upstream, _ = lax.optimization_barrier((hidden, upstream, early_far))
    full_weights = lax.all_gather(weights[0], ("zh", "dp"), axis=0, tiled=True)

    target = table_lookup(placement, route_ids.reshape(-1))
    slot_iota = jnp.arange(2 * plane, dtype=jnp.int32)
    onehot = (target[:, None] == slot_iota[None, :]).astype(jnp.int32)
    rank = jnp.sum((jnp.cumsum(onehot, axis=0) - onehot) * onehot, axis=1)
    position = (target % plane) * slots + (target // plane) * capacity + rank

    send_hidden = jnp.zeros((plane * slots, hidden_width), jnp.bfloat16)
    send_hidden = send_hidden.at[position].set(hidden.reshape(total_rows, hidden_width))
    send_hidden = send_hidden.reshape(plane, slots, hidden_width)
    got_hidden = lax.all_to_all(send_hidden, "p", split_axis=0, concat_axis=0, tiled=True)
    scaled = (route_probs[..., None] * upstream[:, None, :].astype(jnp.float32)).astype(
        jnp.bfloat16
    )
    send_grads = jnp.zeros((plane * slots, width), jnp.bfloat16)
    send_grads = send_grads.at[position].set(scaled.reshape(total_rows, width))
    send_grads = send_grads.reshape(plane, slots, width)
    got_grads = lax.all_to_all(send_grads, "p", split_axis=0, concat_axis=0, tiled=True)

    flat_hidden = got_hidden.reshape(plane * slots, hidden_width)
    flat_grads = got_grads.reshape(plane * slots, width)
    half = (jnp.arange(plane * slots, dtype=jnp.int32) // capacity % 2)[:, None]
    zero = jnp.zeros_like(flat_hidden)
    spread = jnp.concatenate(
        [jnp.where(half == 0, flat_hidden, zero), jnp.where(half == 1, flat_hidden, zero)], axis=1
    )
    new_half = half ^ flip_mine
    spread_new = jnp.concatenate(
        [jnp.where(new_half == 0, flat_hidden, zero), jnp.where(new_half == 1, flat_hidden, zero)],
        axis=1,
    )
    partial = lax.dot_general(
        spread_new, flat_grads, (((0,), (0,)), ((), ())), preferred_element_type=jnp.float32
    ).astype(jnp.bfloat16)
    gradient = lax.psum_scatter(
        partial, ("zh", "dp"), scatter_dimension=0, tiled=True
    )
    full_weights, _ = lax.optimization_barrier((full_weights, partial))

    terms = jnp.dot(spread, full_weights, preferred_element_type=jnp.float32).astype(jnp.bfloat16)
    back_terms = lax.all_to_all(
        terms.reshape(plane, slots, width), "p", split_axis=0, concat_axis=0, tiled=True
    )
    both = lax.dot_general(
        flat_grads, full_weights, (((1,), (1,)), ((), ())), preferred_element_type=jnp.float32
    ).astype(jnp.bfloat16)
    row_grads = jnp.where(half == 0, both[:, :hidden_width], both[:, hidden_width:])
    back_grads = lax.all_to_all(
        row_grads.reshape(plane, slots, hidden_width), "p", split_axis=0, concat_axis=0, tiled=True
    )
    expert_terms = back_terms.reshape(plane * slots, width)[position].reshape(
        tokens_here, chosen, width
    )
    layer_out = jnp.sum(route_probs[..., None] * expert_terms.astype(jnp.float32), axis=1).astype(
        jnp.bfloat16
    )
    hidden_grads = back_grads.reshape(plane * slots, hidden_width)[position].reshape(
        tokens_here, chosen, hidden_width
    )

    late_blocks, _, _ = lax.optimization_barrier((spread_blocks[:, cut:], terms, row_grads))
    late_far = cross(late_blocks)
    far = jnp.concatenate([early_far, late_far], axis=1).reshape(plane, mine, rows_dp, LANES)
    far = lax.all_to_all(far, "p", split_axis=0, concat_axis=0, tiled=True)
    old_half = my_half ^ flip_mine
    row_block = old_half * (hidden_width // rows_dp) + my_dp
    weight_here, first_here, second_here = state_at_home(
        row_block, flip_mine, full_weights, moment1, moment2, far.reshape(moment_blocks.shape)
    )
    new_w, new_first, new_second = adam_update(
        weight_here, first_here, second_here, gradient[None].astype(jnp.float32)
    )
    return (layer_out, hidden_grads, new_w, new_first, new_second)


def solution(mesh):
    n_dp, n_expert = mesh.shape["dp"], mesh.shape["expert"]
    mesh = Mesh(mesh.devices.reshape(n_dp, 2, n_expert // 2), ("dp", "zh", "p"))
    tokens, experts = ("dp", "zh", "p"), ("zh", "p")
    in_specs = (
        P(tokens, None),
        P(tokens, None),
        P(tokens, None, None),
        P(tokens, None),
        P(),
        P(),
        P(experts, "dp", None),
        P(experts, "dp", None),
        P(experts, "dp", None),
    )
    out_specs = (
        P(tokens, None),
        P(tokens, None, None),
        P(experts, "dp", None),
        P(experts, "dp", None),
        P(experts, "dp", None),
    )
    return jax.shard_map(shards, mesh=mesh, in_specs=in_specs, out_specs=out_specs, check_vma=False)
```

```python
import jax
import jax.numpy as jnp
from jax import lax
from jax.experimental import pallas as pl
from jax.experimental.pallas import tpu as pltpu
from jax.sharding import Mesh, PartitionSpec as P

decay_one = 0.9
decay_two = 0.95
learn_rate = 0.01
bias_one = 1.0 - 0.9**10
bias_two = 1.0 - 0.95**10
epsilon = 1e-08


LANES, STEP = 128, 4
PARTS = (4, 8, 10, 12, 13, 14, 15, 16, 17, 18, 19, 20, 21, 22, 24, 26, 28, 32)


def adam_update(weight, decayed_first, decayed_second, gradient):
    new_first = decayed_first + (1.0 - decay_one) * gradient
    new_second = decayed_second + (1.0 - decay_two) * gradient * gradient
    spread = jnp.sqrt(new_second * (1.0 / bias_two)) + epsilon
    step_size = new_first * (learn_rate / bias_one) / spread
    return ((weight.astype(jnp.float32) - step_size).astype(jnp.bfloat16), new_first, new_second)


def pack_kernel(first_ref, second_ref, out_ref):
    for block in range(out_ref.shape[1]):
        columns = pl.ds(block * LANES, LANES)
        out_ref[0, block] = first_ref[0, :, columns].astype(jnp.bfloat16)
        out_ref[1, block] = second_ref[0, :, columns].astype(jnp.bfloat16)


def pack_moments(first, second):
    _, rows, width = first.shape
    blocks = width // LANES
    step = STEP if blocks % STEP == 0 else 1
    moment = pl.BlockSpec((1, rows, step * LANES), lambda i: (0, 0, i))
    return pl.pallas_call(
        pack_kernel,
        grid=(blocks // step,),
        in_specs=[moment, moment],
        out_specs=pl.BlockSpec((2, step, rows, LANES), lambda i: (0, i, 0, 0)),
        out_shape=jax.ShapeDtypeStruct((2, blocks, rows, LANES), jnp.bfloat16),
    )(first, second)


def home_kernel(where_ref, weight_ref, first_ref, second_ref, far_ref, w_ref, m_ref, v_ref):
    moved = where_ref[1] == 1
    w_ref[0] = weight_ref[...]
    for block in range(far_ref.shape[1]):
        columns = pl.ds(block * LANES, LANES)
        first = jnp.where(moved, far_ref[0, block].astype(jnp.float32), first_ref[0, :, columns])
        second = jnp.where(moved, far_ref[1, block].astype(jnp.float32), second_ref[0, :, columns])
        m_ref[0, :, columns] = decay_one * first
        v_ref[0, :, columns] = decay_two * second


def state_at_home(row_block, moved, full_weights, first, second, far):
    _, rows, width = first.shape
    blocks = width // LANES
    step = STEP if blocks % STEP == 0 else 1
    state = pl.BlockSpec((1, rows, step * LANES), lambda i, where: (0, 0, i))
    grid_spec = pltpu.PrefetchScalarGridSpec(
        num_scalar_prefetch=1,
        grid=(blocks // step,),
        in_specs=[
            pl.BlockSpec((rows, step * LANES), lambda i, where: (where[0], i)),
            state,
            state,
            pl.BlockSpec((2, step, rows, LANES), lambda i, where: (0, i, 0, 0)),
        ],
        out_specs=[state, state, state],
    )
    return pl.pallas_call(
        home_kernel,
        grid_spec=grid_spec,
        out_shape=[
            jax.ShapeDtypeStruct(first.shape, jnp.bfloat16),
            jax.ShapeDtypeStruct(first.shape, jnp.float32),
            jax.ShapeDtypeStruct(first.shape, jnp.float32),
        ],
    )(jnp.stack([row_block, moved]), full_weights, first, second, far)


def table_lookup(lookup_table, positions):
    iota_slots = jnp.arange(lookup_table.shape[0], dtype=jnp.int32)
    matches = positions[..., None] == iota_slots
    return jnp.sum(jnp.where(matches, lookup_table, 0), axis=-1)


def shards(
    route_ids, route_probs, hidden, upstream, placement, swap_flags, weights, moment1, moment2
):
    plane = lax.axis_size("p")
    my_half, my_place, my_dp = lax.axis_index("zh"), lax.axis_index("p"), lax.axis_index("dp")
    tokens_here, chosen = route_ids.shape
    width = upstream.shape[1]
    hidden_width = hidden.shape[2]
    rows_dp = weights.shape[1]
    total_rows = tokens_here * chosen
    capacity = total_rows // plane
    slots = 2 * capacity
    flip_mine = table_lookup(swap_flags, my_place)

    plane_flags = swap_flags[:plane]
    order = jnp.cumsum(plane_flags) - 1
    trading = order[-1] + 1
    lines = jnp.arange(plane, dtype=jnp.int32)
    taken = (order[None, :] == lines[:, None]) & (plane_flags[None, :] == 1)
    nth = jnp.sum(jnp.where(taken, lines[None, :], 0), axis=1)
    order = jnp.maximum(order, 0)
    sizes = sorted({max(1, plane * part // 32) for part in PARTS})
    chosen_size = sum((trading > size).astype(jnp.int32) for size in sizes[:-1])

    def crossing(size):
        def branch(blocks):
            packed = jnp.take(blocks, nth[:size], axis=0, mode="clip")
            packed = lax.ppermute(packed, "zh", [(0, 1), (1, 0)])
            return jnp.take(packed, order, axis=0, mode="clip")

        return branch

    def cross(blocks):
        return lax.switch(chosen_size, [crossing(size) for size in sizes], blocks)

    moment_blocks = pack_moments(moment1, moment2)
    spread_blocks = lax.all_to_all(
        moment_blocks.reshape(plane, -1, rows_dp, LANES), "p", split_axis=0, concat_axis=0, tiled=True
    )
    mine = spread_blocks.shape[1]
    spread_blocks = spread_blocks.reshape(plane, mine * rows_dp, LANES)
    cut = mine * rows_dp // 2
    hidden, _ = lax.optimization_barrier((hidden, spread_blocks))
    upstream, _ = lax.optimization_barrier((upstream, spread_blocks))
    full_weights = lax.all_gather(weights[0], ("zh", "dp"), axis=0, tiled=True)

    target = table_lookup(placement, route_ids.reshape(-1))
    slot_iota = jnp.arange(2 * plane, dtype=jnp.int32)
    onehot = (target[:, None] == slot_iota[None, :]).astype(jnp.int32)
    rank = jnp.sum((jnp.cumsum(onehot, axis=0) - onehot) * onehot, axis=1)
    position = (target % plane) * slots + (target // plane) * capacity + rank

    send_hidden = jnp.zeros((plane * slots, hidden_width), jnp.bfloat16)
    send_hidden = send_hidden.at[position].set(hidden.reshape(total_rows, hidden_width))
    send_hidden = send_hidden.reshape(plane, slots, hidden_width)
    got_hidden = lax.all_to_all(send_hidden, "p", split_axis=0, concat_axis=0, tiled=True)
    scaled = (route_probs[..., None] * upstream[:, None, :].astype(jnp.float32)).astype(
        jnp.bfloat16
    )
    send_grads = jnp.zeros((plane * slots, width), jnp.bfloat16)
    send_grads = send_grads.at[position].set(scaled.reshape(total_rows, width))
    send_grads = send_grads.reshape(plane, slots, width)

    early_blocks, send_grads, _ = lax.optimization_barrier((spread_blocks[:, :cut], send_grads, got_hidden))
    early_far = cross(early_blocks)
    got_grads = lax.all_to_all(send_grads, "p", split_axis=0, concat_axis=0, tiled=True)
    got_grads, _ = lax.optimization_barrier((got_grads, early_far))
    flat_hidden = got_hidden.reshape(plane * slots, hidden_width)
    flat_grads = got_grads.reshape(plane * slots, width)
    half = (jnp.arange(plane * slots, dtype=jnp.int32) // capacity % 2)[:, None]
    zero = jnp.zeros_like(flat_hidden)
    spread = jnp.concatenate(
        [jnp.where(half == 0, flat_hidden, zero), jnp.where(half == 1, flat_hidden, zero)], axis=1
    )
    new_half = half ^ flip_mine
    spread_new = jnp.concatenate(
        [jnp.where(new_half == 0, flat_hidden, zero), jnp.where(new_half == 1, flat_hidden, zero)],
        axis=1,
    )
    partial = lax.dot_general(
        spread_new, flat_grads, (((0,), (0,)), ((), ())), preferred_element_type=jnp.float32
    ).astype(jnp.bfloat16)
    gradient = lax.psum_scatter(
        partial, ("zh", "dp"), scatter_dimension=0, tiled=True
    )
    full_weights, _ = lax.optimization_barrier((full_weights, partial))

    terms = jnp.dot(spread, full_weights, preferred_element_type=jnp.float32).astype(jnp.bfloat16)
    back_terms = lax.all_to_all(
        terms.reshape(plane, slots, width), "p", split_axis=0, concat_axis=0, tiled=True
    )
    both = lax.dot_general(
        flat_grads, full_weights, (((1,), (1,)), ((), ())), preferred_element_type=jnp.float32
    ).astype(jnp.bfloat16)
    row_grads = jnp.where(half == 0, both[:, :hidden_width], both[:, hidden_width:])
    back_grads = lax.all_to_all(
        row_grads.reshape(plane, slots, hidden_width), "p", split_axis=0, concat_axis=0, tiled=True
    )
    late_blocks, _, _ = lax.optimization_barrier((spread_blocks[:, cut:], terms, row_grads))
    late_far = cross(late_blocks)
    far = jnp.concatenate([early_far, late_far], axis=1).reshape(plane, mine, rows_dp, LANES)
    far, back_terms = lax.optimization_barrier((far, back_terms))
    far = lax.all_to_all(far, "p", split_axis=0, concat_axis=0, tiled=True)
    old_half = my_half ^ flip_mine
    row_block = old_half * (hidden_width // rows_dp) + my_dp
    weight_here, first_here, second_here = state_at_home(
        row_block, flip_mine, full_weights, moment1, moment2, far.reshape(moment_blocks.shape)
    )
    new_w, new_first, new_second = adam_update(
        weight_here, first_here, second_here, gradient[None].astype(jnp.float32)
    )
    expert_terms = back_terms.reshape(plane * slots, width)[position].reshape(
        tokens_here, chosen, width
    )
    layer_out = jnp.sum(route_probs[..., None] * expert_terms.astype(jnp.float32), axis=1).astype(
        jnp.bfloat16
    )
    hidden_grads = back_grads.reshape(plane * slots, hidden_width)[position].reshape(
        tokens_here, chosen, hidden_width
    )

    return (layer_out, hidden_grads, new_w, new_first, new_second)


def solution(mesh):
    n_dp, n_expert = mesh.shape["dp"], mesh.shape["expert"]
    mesh = Mesh(mesh.devices.reshape(n_dp, 2, n_expert // 2), ("dp", "zh", "p"))
    tokens, experts = ("dp", "zh", "p"), ("zh", "p")
    in_specs = (
        P(tokens, None),
        P(tokens, None),
        P(tokens, None, None),
        P(tokens, None),
        P(),
        P(),
        P(experts, "dp", None),
        P(experts, "dp", None),
        P(experts, "dp", None),
    )
    out_specs = (
        P(tokens, None),
        P(tokens, None, None),
        P(experts, "dp", None),
        P(experts, "dp", None),
        P(experts, "dp", None),
    )
    return jax.shard_map(shards, mesh=mesh, in_specs=in_specs, out_specs=out_specs, check_vma=False)
```

```python
import jax
import jax.numpy as jnp
from jax import lax
from jax.experimental import pallas as pl
from jax.experimental.pallas import tpu as pltpu
from jax.sharding import Mesh, PartitionSpec as P

decay_one = 0.9
decay_two = 0.95
learn_rate = 0.01
bias_one = 1.0 - 0.9**10
bias_two = 1.0 - 0.95**10
epsilon = 1e-08


LANES, STEP = 128, 4
PARTS = (4, 8, 10, 12, 13, 14, 15, 16, 17, 18, 19, 20, 21, 22, 24, 26, 28, 32)


def adam_update(weight, decayed_first, decayed_second, gradient):
    new_first = decayed_first + (1.0 - decay_one) * gradient
    new_second = decayed_second + (1.0 - decay_two) * gradient * gradient
    spread = jnp.sqrt(new_second * (1.0 / bias_two)) + epsilon
    step_size = new_first * (learn_rate / bias_one) / spread
    return ((weight.astype(jnp.float32) - step_size).astype(jnp.bfloat16), new_first, new_second)


def pack_kernel(first_ref, second_ref, out_ref):
    for block in range(out_ref.shape[1]):
        columns = pl.ds(block * LANES, LANES)
        out_ref[0, block] = first_ref[0, :, columns].astype(jnp.bfloat16)
        out_ref[1, block] = second_ref[0, :, columns].astype(jnp.bfloat16)


def pack_moments(first, second):
    _, rows, width = first.shape
    blocks = width // LANES
    step = STEP if blocks % STEP == 0 else 1
    moment = pl.BlockSpec((1, rows, step * LANES), lambda i: (0, 0, i))
    return pl.pallas_call(
        pack_kernel,
        grid=(blocks // step,),
        in_specs=[moment, moment],
        out_specs=pl.BlockSpec((2, step, rows, LANES), lambda i: (0, i, 0, 0)),
        out_shape=jax.ShapeDtypeStruct((2, blocks, rows, LANES), jnp.bfloat16),
    )(first, second)


def home_kernel(
    where_ref, weight_ref, first_ref, second_ref, early_ref, late_ref, w_ref, m_ref, v_ref
):
    moved = where_ref[1] == 1
    w_ref[0] = weight_ref[...]
    cut = early_ref.shape[2]
    for block in range(early_ref.shape[1]):
        columns = pl.ds(block * LANES, LANES)
        for rows, far_ref in ((pl.ds(0, cut), early_ref), (pl.ds(cut, late_ref.shape[2]), late_ref)):
            far_first = far_ref[0, block].astype(jnp.float32)
            far_second = far_ref[1, block].astype(jnp.float32)
            first = jnp.where(moved, far_first, first_ref[0, rows, columns])
            second = jnp.where(moved, far_second, second_ref[0, rows, columns])
            m_ref[0, rows, columns] = decay_one * first
            v_ref[0, rows, columns] = decay_two * second


def state_at_home(row_block, moved, full_weights, first, second, early, late):
    _, rows, width = first.shape
    blocks = width // LANES
    step = STEP if blocks % STEP == 0 else 1
    state = pl.BlockSpec((1, rows, step * LANES), lambda i, where: (0, 0, i))

    def far(part):
        return pl.BlockSpec((2, step, part.shape[2], LANES), lambda i, where: (0, i, 0, 0))

    grid_spec = pltpu.PrefetchScalarGridSpec(
        num_scalar_prefetch=1,
        grid=(blocks // step,),
        in_specs=[
            pl.BlockSpec((rows, step * LANES), lambda i, where: (where[0], i)),
            state,
            state,
            far(early),
            far(late),
        ],
        out_specs=[state, state, state],
    )
    return pl.pallas_call(
        home_kernel,
        grid_spec=grid_spec,
        out_shape=[
            jax.ShapeDtypeStruct(first.shape, jnp.bfloat16),
            jax.ShapeDtypeStruct(first.shape, jnp.float32),
            jax.ShapeDtypeStruct(first.shape, jnp.float32),
        ],
    )(jnp.stack([row_block, moved]), full_weights, first, second, early, late)


def table_lookup(lookup_table, positions):
    iota_slots = jnp.arange(lookup_table.shape[0], dtype=jnp.int32)
    matches = positions[..., None] == iota_slots
    return jnp.sum(jnp.where(matches, lookup_table, 0), axis=-1)


def shards(
    route_ids, route_probs, hidden, upstream, placement, swap_flags, weights, moment1, moment2
):
    plane = lax.axis_size("p")
    my_half, my_place, my_dp = lax.axis_index("zh"), lax.axis_index("p"), lax.axis_index("dp")
    tokens_here, chosen = route_ids.shape
    width = upstream.shape[1]
    hidden_width = hidden.shape[2]
    rows_dp = weights.shape[1]
    total_rows = tokens_here * chosen
    capacity = total_rows // plane
    slots = 2 * capacity
    flip_mine = table_lookup(swap_flags, my_place)

    plane_flags = swap_flags[:plane]
    order = jnp.cumsum(plane_flags) - 1
    trading = order[-1] + 1
    lines = jnp.arange(plane, dtype=jnp.int32)
    taken = (order[None, :] == lines[:, None]) & (plane_flags[None, :] == 1)
    nth = jnp.sum(jnp.where(taken, lines[None, :], 0), axis=1)
    order = jnp.maximum(order, 0)
    sizes = sorted({max(1, plane * part // 32) for part in PARTS})
    chosen_size = sum((trading > size).astype(jnp.int32) for size in sizes[:-1])

    def crossing(size):
        def branch(blocks):
            packed = jnp.take(blocks, nth[:size], axis=0, mode="clip")
            packed = lax.ppermute(packed, "zh", [(0, 1), (1, 0)])
            return jnp.take(packed, order, axis=0, mode="clip")

        return branch

    def cross(blocks):
        return lax.switch(chosen_size, [crossing(size) for size in sizes], blocks)

    moment_blocks = pack_moments(moment1, moment2)
    spread_blocks = lax.all_to_all(
        moment_blocks.reshape(plane, -1, rows_dp, LANES), "p", split_axis=0, concat_axis=0, tiled=True
    )
    spread_blocks = spread_blocks.reshape(plane, rows_dp, LANES)
    cut = rows_dp * 4 // 12 // 8 * 8
    hidden, _ = lax.optimization_barrier((hidden, spread_blocks))
    upstream, _ = lax.optimization_barrier((upstream, spread_blocks))
    full_weights = lax.all_gather(weights[0], ("zh", "dp"), axis=0, tiled=True)

    target = table_lookup(placement, route_ids.reshape(-1))
    slot_iota = jnp.arange(2 * plane, dtype=jnp.int32)
    onehot = (target[:, None] == slot_iota[None, :]).astype(jnp.int32)
    rank = jnp.sum((jnp.cumsum(onehot, axis=0) - onehot) * onehot, axis=1)
    position = (target % plane) * slots + (target // plane) * capacity + rank

    send_hidden = jnp.zeros((plane * slots, hidden_width), jnp.bfloat16)
    send_hidden = send_hidden.at[position].set(hidden.reshape(total_rows, hidden_width))
    send_hidden = send_hidden.reshape(plane, slots, hidden_width)
    got_hidden = lax.all_to_all(send_hidden, "p", split_axis=0, concat_axis=0, tiled=True)
    scaled = (route_probs[..., None] * upstream[:, None, :].astype(jnp.float32)).astype(
        jnp.bfloat16
    )
    send_grads = jnp.zeros((plane * slots, width), jnp.bfloat16)
    send_grads = send_grads.at[position].set(scaled.reshape(total_rows, width))
    send_grads = send_grads.reshape(plane, slots, width)

    early_blocks, send_grads, _ = lax.optimization_barrier((spread_blocks[:, :cut], send_grads, got_hidden))
    early_far = cross(early_blocks)
    got_grads = lax.all_to_all(send_grads, "p", split_axis=0, concat_axis=0, tiled=True)
    got_grads, _ = lax.optimization_barrier((got_grads, early_far))
    flat_hidden = got_hidden.reshape(plane * slots, hidden_width)
    flat_grads = got_grads.reshape(plane * slots, width)
    half = (jnp.arange(plane * slots, dtype=jnp.int32) // capacity % 2)[:, None]
    zero = jnp.zeros_like(flat_hidden)
    spread = jnp.concatenate(
        [jnp.where(half == 0, flat_hidden, zero), jnp.where(half == 1, flat_hidden, zero)], axis=1
    )
    new_half = half ^ flip_mine
    spread_new = jnp.concatenate(
        [jnp.where(new_half == 0, flat_hidden, zero), jnp.where(new_half == 1, flat_hidden, zero)],
        axis=1,
    )
    partial = lax.dot_general(
        spread_new, flat_grads, (((0,), (0,)), ((), ())), preferred_element_type=jnp.float32
    ).astype(jnp.bfloat16)
    gradient = lax.psum_scatter(
        partial, ("zh", "dp"), scatter_dimension=0, tiled=True
    )
    early_far, _ = lax.optimization_barrier((early_far, partial))
    early_home = lax.all_to_all(early_far, "p", split_axis=0, concat_axis=0, tiled=True)
    late_blocks, full_weights, _ = lax.optimization_barrier((spread_blocks[:, cut:], full_weights, early_home))
    late_far = cross(late_blocks)
    full_weights, _ = lax.optimization_barrier((full_weights, late_far))

    terms = jnp.dot(spread, full_weights, preferred_element_type=jnp.float32).astype(jnp.bfloat16)
    back_terms = lax.all_to_all(
        terms.reshape(plane, slots, width), "p", split_axis=0, concat_axis=0, tiled=True
    )
    both = lax.dot_general(
        flat_grads, full_weights, (((1,), (1,)), ((), ())), preferred_element_type=jnp.float32
    ).astype(jnp.bfloat16)
    row_grads = jnp.where(half == 0, both[:, :hidden_width], both[:, hidden_width:])
    back_grads = lax.all_to_all(
        row_grads.reshape(plane, slots, hidden_width), "p", split_axis=0, concat_axis=0, tiled=True
    )
    late_far, _ = lax.optimization_barrier((late_far, back_grads))
    late_home = lax.all_to_all(late_far, "p", split_axis=0, concat_axis=0, tiled=True)
    old_half = my_half ^ flip_mine
    row_block = old_half * (hidden_width // rows_dp) + my_dp
    weight_here, first_here, second_here = state_at_home(
        row_block,
        flip_mine,
        full_weights,
        moment1,
        moment2,
        early_home.reshape(2, plane // 2, cut, LANES),
        late_home.reshape(2, plane // 2, rows_dp - cut, LANES),
    )
    new_w, new_first, new_second = adam_update(
        weight_here, first_here, second_here, gradient[None].astype(jnp.float32)
    )
    expert_terms = back_terms.reshape(plane * slots, width)[position].reshape(
        tokens_here, chosen, width
    )
    layer_out = jnp.sum(route_probs[..., None] * expert_terms.astype(jnp.float32), axis=1).astype(
        jnp.bfloat16
    )
    hidden_grads = back_grads.reshape(plane * slots, hidden_width)[position].reshape(
        tokens_here, chosen, hidden_width
    )

    return (layer_out, hidden_grads, new_w, new_first, new_second)


def solution(mesh):
    n_dp, n_expert = mesh.shape["dp"], mesh.shape["expert"]
    mesh = Mesh(mesh.devices.reshape(n_dp, 2, n_expert // 2), ("dp", "zh", "p"))
    tokens, experts = ("dp", "zh", "p"), ("zh", "p")
    in_specs = (
        P(tokens, None),
        P(tokens, None),
        P(tokens, None, None),
        P(tokens, None),
        P(),
        P(),
        P(experts, "dp", None),
        P(experts, "dp", None),
        P(experts, "dp", None),
    )
    out_specs = (
        P(tokens, None),
        P(tokens, None, None),
        P(experts, "dp", None),
        P(experts, "dp", None),
        P(experts, "dp", None),
    )
    return jax.shard_map(shards, mesh=mesh, in_specs=in_specs, out_specs=out_specs, check_vma=False)
```

```python
import jax
import jax.numpy as jnp
from jax import lax
from jax.experimental import pallas as pl
from jax.experimental.pallas import tpu as pltpu
from jax.sharding import Mesh, PartitionSpec as P

decay_one = 0.9
decay_two = 0.95
learn_rate = 0.01
bias_one = 1.0 - 0.9**10
bias_two = 1.0 - 0.95**10
epsilon = 1e-08


LANES, STEP = 128, 4
PARTS = (4, 8, 10, 12, 13, 14, 15, 16, 17, 18, 19, 20, 21, 22, 24, 26, 28, 32)


def adam_update(weight, decayed_first, decayed_second, gradient):
    new_first = decayed_first + (1.0 - decay_one) * gradient
    new_second = decayed_second + (1.0 - decay_two) * gradient * gradient
    spread = jnp.sqrt(new_second * (1.0 / bias_two)) + epsilon
    step_size = new_first * (learn_rate / bias_one) / spread
    return ((weight.astype(jnp.float32) - step_size).astype(jnp.bfloat16), new_first, new_second)


def pack_kernel(first_ref, second_ref, out_ref):
    for block in range(out_ref.shape[1]):
        columns = pl.ds(block * LANES, LANES)
        out_ref[0, block] = first_ref[0, :, columns].astype(jnp.bfloat16)
        out_ref[1, block] = second_ref[0, :, columns].astype(jnp.bfloat16)


def pack_moments(first, second):
    _, rows, width = first.shape
    blocks = width // LANES
    step = STEP if blocks % STEP == 0 else 1
    moment = pl.BlockSpec((1, rows, step * LANES), lambda i: (0, 0, i))
    return pl.pallas_call(
        pack_kernel,
        grid=(blocks // step,),
        in_specs=[moment, moment],
        out_specs=pl.BlockSpec((2, step, rows, LANES), lambda i: (0, i, 0, 0)),
        out_shape=jax.ShapeDtypeStruct((2, blocks, rows, LANES), jnp.bfloat16),
    )(first, second)


def home_kernel(
    where_ref, weight_ref, first_ref, second_ref, early_ref, late_ref, w_ref, m_ref, v_ref
):
    moved = where_ref[1] == 1
    w_ref[0] = weight_ref[...]
    cut = early_ref.shape[2]
    for block in range(early_ref.shape[1]):
        columns = pl.ds(block * LANES, LANES)
        for rows, far_ref in ((pl.ds(0, cut), early_ref), (pl.ds(cut, late_ref.shape[2]), late_ref)):
            far_first = far_ref[0, block].astype(jnp.float32)
            far_second = far_ref[1, block].astype(jnp.float32)
            first = jnp.where(moved, far_first, first_ref[0, rows, columns])
            second = jnp.where(moved, far_second, second_ref[0, rows, columns])
            m_ref[0, rows, columns] = decay_one * first
            v_ref[0, rows, columns] = decay_two * second


def state_at_home(row_block, moved, full_weights, first, second, early, late):
    _, rows, width = first.shape
    blocks = width // LANES
    step = STEP if blocks % STEP == 0 else 1
    state = pl.BlockSpec((1, rows, step * LANES), lambda i, where: (0, 0, i))

    def far(part):
        return pl.BlockSpec((2, step, part.shape[2], LANES), lambda i, where: (0, i, 0, 0))

    grid_spec = pltpu.PrefetchScalarGridSpec(
        num_scalar_prefetch=1,
        grid=(blocks // step,),
        in_specs=[
            pl.BlockSpec((rows, step * LANES), lambda i, where: (where[0], i)),
            state,
            state,
            far(early),
            far(late),
        ],
        out_specs=[state, state, state],
    )
    return pl.pallas_call(
        home_kernel,
        grid_spec=grid_spec,
        out_shape=[
            jax.ShapeDtypeStruct(first.shape, jnp.bfloat16),
            jax.ShapeDtypeStruct(first.shape, jnp.float32),
            jax.ShapeDtypeStruct(first.shape, jnp.float32),
        ],
    )(jnp.stack([row_block, moved]), full_weights, first, second, early, late)


def table_lookup(lookup_table, positions):
    iota_slots = jnp.arange(lookup_table.shape[0], dtype=jnp.int32)
    matches = positions[..., None] == iota_slots
    return jnp.sum(jnp.where(matches, lookup_table, 0), axis=-1)


def shards(
    route_ids, route_probs, hidden, upstream, placement, swap_flags, weights, moment1, moment2
):
    plane = lax.axis_size("p")
    my_half, my_place, my_dp = lax.axis_index("zh"), lax.axis_index("p"), lax.axis_index("dp")
    tokens_here, chosen = route_ids.shape
    width = upstream.shape[1]
    hidden_width = hidden.shape[2]
    rows_dp = weights.shape[1]
    total_rows = tokens_here * chosen
    capacity = total_rows // plane
    slots = 2 * capacity
    flip_mine = table_lookup(swap_flags, my_place)

    plane_flags = swap_flags[:plane]
    order = jnp.cumsum(plane_flags) - 1
    trading = order[-1] + 1
    lines = jnp.arange(plane, dtype=jnp.int32)
    taken = (order[None, :] == lines[:, None]) & (plane_flags[None, :] == 1)
    nth = jnp.sum(jnp.where(taken, lines[None, :], 0), axis=1)
    order = jnp.maximum(order, 0)
    sizes = sorted({max(1, plane * part // 32) for part in PARTS})
    chosen_size = sum((trading > size).astype(jnp.int32) for size in sizes[:-1])

    def crossing(size):
        def branch(blocks):
            packed = jnp.take(blocks, nth[:size], axis=0, mode="clip")
            packed = lax.ppermute(packed, "zh", [(0, 1), (1, 0)])
            return jnp.take(packed, order, axis=0, mode="clip")

        return branch

    def cross(blocks):
        return lax.switch(chosen_size, [crossing(size) for size in sizes], blocks)

    moment_blocks = pack_moments(moment1, moment2)
    spread_blocks = lax.all_to_all(
        moment_blocks.reshape(plane, -1, rows_dp, LANES), "p", split_axis=0, concat_axis=0, tiled=True
    )
    spread_blocks = spread_blocks.reshape(plane, rows_dp, LANES)
    cut = rows_dp * 4 // 12 // 8 * 8
    hidden, _ = lax.optimization_barrier((hidden, spread_blocks))
    upstream, _ = lax.optimization_barrier((upstream, spread_blocks))
    full_weights = lax.all_gather(weights[0], ("zh", "dp"), axis=0, tiled=True)

    target = table_lookup(placement, route_ids.reshape(-1))
    slot_iota = jnp.arange(2 * plane, dtype=jnp.int32)
    onehot = (target[:, None] == slot_iota[None, :]).astype(jnp.int32)
    rank = jnp.sum((jnp.cumsum(onehot, axis=0) - onehot) * onehot, axis=1)
    position = (target % plane) * slots + (target // plane) * capacity + rank

    send_hidden = jnp.zeros((plane * slots, hidden_width), jnp.bfloat16)
    send_hidden = send_hidden.at[position].set(hidden.reshape(total_rows, hidden_width))
    send_hidden = send_hidden.reshape(plane, slots, hidden_width)
    got_hidden = lax.all_to_all(send_hidden, "p", split_axis=0, concat_axis=0, tiled=True)
    scaled = (route_probs[..., None] * upstream[:, None, :].astype(jnp.float32)).astype(
        jnp.bfloat16
    )
    send_grads = jnp.zeros((plane * slots, width), jnp.bfloat16)
    send_grads = send_grads.at[position].set(scaled.reshape(total_rows, width))
    send_grads = send_grads.reshape(plane, slots, width)

    early_blocks, send_grads, _ = lax.optimization_barrier((spread_blocks[:, :cut], send_grads, got_hidden))
    early_far = cross(early_blocks)
    got_grads = lax.all_to_all(send_grads, "p", split_axis=0, concat_axis=0, tiled=True)
    got_grads, _ = lax.optimization_barrier((got_grads, early_far))
    flat_hidden = got_hidden.reshape(plane * slots, hidden_width)
    flat_grads = got_grads.reshape(plane * slots, width)
    half = (jnp.arange(plane * slots, dtype=jnp.int32) // capacity % 2)[:, None]
    zero = jnp.zeros_like(flat_hidden)
    spread = jnp.concatenate(
        [jnp.where(half == 0, flat_hidden, zero), jnp.where(half == 1, flat_hidden, zero)], axis=1
    )
    new_half = half ^ flip_mine
    spread_new = jnp.concatenate(
        [jnp.where(new_half == 0, flat_hidden, zero), jnp.where(new_half == 1, flat_hidden, zero)],
        axis=1,
    )
    partial = lax.dot_general(
        spread_new, flat_grads, (((0,), (0,)), ((), ())), preferred_element_type=jnp.float32
    ).astype(jnp.bfloat16)
    gradient = lax.psum_scatter(
        partial, ("zh", "dp"), scatter_dimension=0, tiled=True
    )
    early_far, _ = lax.optimization_barrier((early_far, partial))
    early_home = lax.all_to_all(early_far, "p", split_axis=0, concat_axis=0, tiled=True)
    late_blocks, full_weights, _ = lax.optimization_barrier((spread_blocks[:, cut:], full_weights, early_home))
    late_far = cross(late_blocks)
    full_weights, _ = lax.optimization_barrier((full_weights, late_far))
    late_home = lax.all_to_all(late_far, "p", split_axis=0, concat_axis=0, tiled=True)

    terms = jnp.dot(spread, full_weights, preferred_element_type=jnp.float32).astype(jnp.bfloat16)
    both = lax.dot_general(
        flat_grads, full_weights, (((1,), (1,)), ((), ())), preferred_element_type=jnp.float32
    ).astype(jnp.bfloat16)
    row_grads = jnp.where(half == 0, both[:, :hidden_width], both[:, hidden_width:])
    row_grads, _ = lax.optimization_barrier((row_grads, late_home))
    back_grads = lax.all_to_all(
        row_grads.reshape(plane, slots, hidden_width), "p", split_axis=0, concat_axis=0, tiled=True
    )
    terms, _ = lax.optimization_barrier((terms, back_grads))
    back_terms = lax.all_to_all(
        terms.reshape(plane, slots, width), "p", split_axis=0, concat_axis=0, tiled=True
    )
    old_half = my_half ^ flip_mine
    row_block = old_half * (hidden_width // rows_dp) + my_dp
    weight_here, first_here, second_here = state_at_home(
        row_block,
        flip_mine,
        full_weights,
        moment1,
        moment2,
        early_home.reshape(2, plane // 2, cut, LANES),
        late_home.reshape(2, plane // 2, rows_dp - cut, LANES),
    )
    new_w, new_first, new_second = adam_update(
        weight_here, first_here, second_here, gradient[None].astype(jnp.float32)
    )
    expert_terms = back_terms.reshape(plane * slots, width)[position].reshape(
        tokens_here, chosen, width
    )
    layer_out = jnp.sum(route_probs[..., None] * expert_terms.astype(jnp.float32), axis=1).astype(
        jnp.bfloat16
    )
    hidden_grads = back_grads.reshape(plane * slots, hidden_width)[position].reshape(
        tokens_here, chosen, hidden_width
    )

    return (layer_out, hidden_grads, new_w, new_first, new_second)


def solution(mesh):
    n_dp, n_expert = mesh.shape["dp"], mesh.shape["expert"]
    mesh = Mesh(mesh.devices.reshape(n_dp, 2, n_expert // 2), ("dp", "zh", "p"))
    tokens, experts = ("dp", "zh", "p"), ("zh", "p")
    in_specs = (
        P(tokens, None),
        P(tokens, None),
        P(tokens, None, None),
        P(tokens, None),
        P(),
        P(),
        P(experts, "dp", None),
        P(experts, "dp", None),
        P(experts, "dp", None),
    )
    out_specs = (
        P(tokens, None),
        P(tokens, None, None),
        P(experts, "dp", None),
        P(experts, "dp", None),
        P(experts, "dp", None),
    )
    return jax.shard_map(shards, mesh=mesh, in_specs=in_specs, out_specs=out_specs, check_vma=False)
```
